32 devices in a mesh: orient: 8 (over z, y), brow: 2 (over core), bcol: 2 (over x).
Axes of the slice: x: 2, y: 2, z: 4, core: 2. Of those that a mesh axis runs over, the one named last changes fastest.
Arguments:
- volume: float32 [8, 64, 208], P('orient', 'brow', 'bcol'), may hold values from -700 to 700
- template: float32 [24, 24, 24], replicated, may hold values from 0 to 1
- voxel_maps: int32 [8, 13824], P('orient'), may hold values from 0 to 13823, as said below
Outputs:
- best: float32 [8, 64, 208], P('orient', 'brow', 'bcol')
The draws below stay inside these ranges and needn't reach their ends.
Inputs may be any that keep to these rules, and one draw needn't show every extreme that they name: `voxel_maps`: each row holds every number of 0 to 13823 exactly once.
All inputs are finite; a program needn't handle non-finite values.
Results may differ from the reference program's by a relative error of at most 0.00013.
Values sent between devices are 32-bit elements; how exact they have to be, the bound alone decides.
A program may use at most 64 MiB of HBM per device.

```python
import math
import jax
import jax.numpy as jnp
from jax import lax

TS = 24
HALF = 12
VOX = 13824
NZ = 8
NX = 64
NY = 208
ROT = 8


def draw_volume(key, part):
    subkeys = jax.random.split(jax.random.fold_in(key, 17), 3)
    row_scale = jnp.exp(jax.random.uniform(subkeys[1], (NZ, NX, 1), minval=0.0, maxval=math.log(10.0)))
    col_scale = jnp.exp(jax.random.uniform(subkeys[2], (1, 1, NY), minval=0.0, maxval=math.log(10.0)))
    noise_part = jnp.clip(jax.random.normal(subkeys[0], (NZ, NX, NY)), -6.0, 6.0)
    samples = noise_part * row_scale * col_scale
    return samples.astype(jnp.float32)


def cycled_row(row_key):
    identity = jnp.arange(VOX, dtype=jnp.int32)
    order = jax.random.permutation(row_key, identity)
    moved_count = max(VOX // 16, 2)
    moved = order[:moved_count]
    targets = jnp.roll(moved, 1)
    return identity.at[moved].set(targets)


def draw_voxel_maps(key, part):
    row_keys = jax.random.split(jax.random.fold_in(key, 29), ROT)
    return jax.vmap(cycled_row)(row_keys).astype(jnp.int32)


def setup_inputs(seed: int = 0) -> dict:
    streams_of = jax.random.split(jax.random.key(seed), 4)
    volume = draw_volume(jax.random.fold_in(streams_of[3], 71), 0)
    template = jnp.clip(jax.random.uniform(streams_of[1], (TS, TS, TS), jnp.float32, 0.0, 1.0), 0.0, 1.0)
    voxel_maps = draw_voxel_maps(jax.random.fold_in(streams_of[3], 71), 0)
    return dict(volume=volume, template=template, voxel_maps=voxel_maps)


epsilon = 1e-06
floor_share = 0.1

def whiten_window(volume):
    spectrum = jnp.fft.fft(volume, axis=-1)
    power_spec = spectrum.real * spectrum.real + spectrum.imag * spectrum.imag
    smoothed = (jnp.roll(power_spec, 1, axis=-1) + power_spec + jnp.roll(power_spec, -1, axis=-1)) / 3.0
    smoothed = smoothed + floor_share * lax.optimization_barrier(jnp.mean(power_spec, axis=-1, keepdims=True)) + epsilon
    weights = lax.rsqrt(smoothed)
    return jnp.fft.ifft(spectrum * weights, axis=-1).real * math.sqrt(NY)

def reference(volume, template, voxel_maps):
    whitened = whiten_window(volume)
    padded = jnp.pad(whitened, HALF)
    flattened = template.reshape(-1)
    centred = flattened - jnp.mean(flattened)
    normed = centred / jnp.sqrt(jnp.sum(centred * centred) + epsilon)
    full_shape = padded.shape
    volume_spec = jnp.fft.fftn(padded)
    energy = lax.reduce_window(padded * padded, jnp.zeros((), padded.dtype), lax.add, (TS, TS, TS), (1, 1, 1), 'VALID')[:NZ, :NX, :NY]
    scaling = lax.rsqrt(energy / VOX + epsilon)

    def one_rotation(maximum, index_map):
        rotated = normed[index_map].reshape(TS, TS, TS)
        tpl_spec = jnp.fft.fftn(rotated, s=full_shape)
        correlation = jnp.fft.ifftn(volume_spec * jnp.conj(tpl_spec)).real[:NZ, :NX, :NY]
        return (jnp.maximum(maximum, correlation * scaling), None)
    initial = jnp.full((NZ, NX, NY), -jnp.inf, dtype=whitened.dtype)
    maximum, unused = lax.scan(one_rotation, initial, voxel_maps)
    return maximum
```

```python
import math

import numpy as np
import jax
import jax.numpy as jnp
from jax import lax
from jax.experimental import pallas as pl
from jax.experimental.pallas import tpu as pltpu
from jax.sharding import PartitionSpec as P

epsilon = 1e-06
floor_share = 0.1
highest = lax.Precision.HIGHEST
LANES = 128
MESH = pl.DeviceIdType.MESH


def round_up(value, step):
    return -(-value // step) * step


def forward_table(length, parts):
    half = length // 2 + 1
    padded = round_up(half, LANES)
    angles = 2.0 * np.pi * (np.outer(np.arange(length), np.arange(half)) % length) / length
    table = np.zeros((length, 2 * padded))
    table[:, :half] = np.cos(angles)
    table[:, padded : padded + half] = -np.sin(angles)
    return table.reshape(parts, length // parts, 2 * padded).astype(np.float32)


def smoothing_table(length):
    half = length // 2 + 1
    padded = round_up(half, LANES)
    table = np.zeros((padded, padded))
    fold = np.minimum(np.arange(length), length - np.arange(length))
    for k in range(half):
        for shift in (-1, 0, 1):
            table[fold[(k + shift) % length], k] += 1.0 / 3.0
        for other in range(length):
            table[fold[other], k] += floor_share / length
    return table.astype(np.float32)


def windowed_inverse(length, parts, margin):
    half = length // 2 + 1
    padded = round_up(half, LANES)
    width = length // parts
    tables = np.zeros((parts, 2 * padded, width + 2 * margin))
    k = np.arange(half)
    share = np.where((k == 0) | (2 * k == length), 1.0, 2.0)[:, None] / math.sqrt(length)
    for part in range(parts):
        columns = np.arange(width + 2 * margin) + part * width - margin
        inside = (columns >= 0) & (columns < length)
        angles = 2.0 * np.pi * (np.outer(k, columns) % length) / length
        tables[part, :half] = share * np.cos(angles) * inside
        tables[part, padded : padded + half] = -share * np.sin(angles) * inside
    return tables.astype(np.float32)


def packed_dft(count, size):
    k = np.arange(size)
    real = k <= size // 2
    freq = np.where(real, k, k - size // 2)
    angles = 2.0 * np.pi * (np.outer(np.arange(count), freq) % size) / size
    return angles, real, freq


def volume_table(size):
    angles, real, freq = packed_dft(size, size)
    return np.where(real, np.cos(angles), -np.sin(angles)).astype(np.float32)


def template_table(count, size):
    angles, real, freq = packed_dft(count, size)
    straight = np.cos(angles)
    edge = (freq == 0) | (freq == size // 2)
    crossed = np.where(real, -np.sin(angles), np.sin(angles)) * ~edge
    return np.concatenate([straight, crossed], axis=1).astype(np.float32)


def score_table(size, count):
    angles, real, freq = packed_dft(count, size)
    share = np.where((freq == 0) | (freq == size // 2), 1.0, 2.0)
    return (np.where(real, np.cos(angles), -np.sin(angles)) * share / size).T.astype(np.float32)


def box_table(size, count, edge):
    offsets = np.arange(size)[:, None] - np.arange(count)[None, :]
    return ((offsets >= 0) & (offsets < edge)).astype(np.float32)


def dot(a, b):
    return jnp.dot(a, b, precision=highest, preferred_element_type=jnp.float32)


def rotate_kernel(voxels, lead, table_ref, index_ref, dft_ref, straight_ref, crossed_ref, normed, rotated):
    table = table_ref[...]
    rows = table.shape[0]
    flat = lax.broadcasted_iota(jnp.int32, table.shape, 0) * LANES + lax.broadcasted_iota(
        jnp.int32, table.shape, 1
    )
    valid = flat < voxels
    mean = jnp.sum(table, keepdims=True) / voxels
    centred = jnp.where(valid, table - mean, 0.0)
    normed[...] = centred / jnp.sqrt(jnp.sum(centred * centred, keepdims=True) + epsilon)
    edge, width = index_ref.shape
    tiles = [(s, c) for s in range(0, edge, 8) for c in range(0, width, LANES)]
    lows, highs = [], []
    for s, c in tiles:
        index = index_ref[s : s + 8, c : c + LANES]
        lows.append(index & (LANES - 1))
        highs.append(index >> 7)

    def step(h, held):
        row = jnp.broadcast_to(normed[pl.ds(h, 1), :], (8, LANES))
        return tuple(
            jnp.where(high == h, jnp.take_along_axis(row, low, axis=1), value)
            for low, high, value in zip(lows, highs, held)
        )

    zero = jnp.zeros((8, LANES), jnp.float32)
    held = lax.fori_loop(0, rows, step, tuple(zero for _ in tiles))
    for (s, c), value in zip(tiles, held):
        rotated[s : s + 8, c : c + LANES] = value
    spectrum = lax.dot_general(
        rotated[...],
        dft_ref[...],
        (((0,), (0,)), ((), ())),
        precision=highest,
        preferred_element_type=jnp.float32,
    )
    size = spectrum.shape[1] // 2
    if straight_ref.shape[0] > edge:
        straight_ref[...] = jnp.zeros_like(straight_ref)
        crossed_ref[...] = jnp.zeros_like(crossed_ref)
    straight_ref[lead : lead + edge] = spectrum[: edge * edge, :size].reshape(edge, edge, size)
    crossed_ref[lead : lead + edge] = spectrum[: edge * edge, size:].reshape(edge, edge, size)


def match_kernel(
    sizes,
    brick_ref,
    straight_ref,
    crossed_ref,
    forward_ref,
    smoothing_ref,
    inverse_ref,
    volume_dft_ref,
    score_dft_ref,
    box_ref,
    best_ref,
    pencils,
    tall,
    windows,
    spectrum,
    swapped,
    energy,
    totals,
    scores,
    arrived,
    sems1,
    sems2,
    sems3,
):
    orients, brows, bcols, edge, voxels, lead = sizes
    half_edge = edge // 2
    rows, cols = brick_ref.shape[1:]
    tile_rows = windows.shape[1]
    me = lax.axis_index("orient")
    row_id = lax.axis_index("brow")
    col_id = lax.axis_index("bcol")
    group = brows * bcols
    place = row_id * bcols + col_id

    def brick_peer(step):
        other = lax.rem(place + step, group)
        return {"orient": me, "brow": other // bcols, "bcol": lax.rem(other, bcols)}

    def plane_peer(step):
        return {"orient": lax.rem(me + step, orients), "brow": row_id, "bcol": col_id}

    barrier = pltpu.get_barrier_semaphore()
    for step in range(1, group):
        pl.semaphore_signal(barrier, inc=1, device_id=brick_peer(step), device_id_type=MESH)
    for step in range(1, orients):
        pl.semaphore_signal(barrier, inc=1, device_id=plane_peer(step), device_id_type=MESH)
    pl.semaphore_wait(barrier, group + orients - 2)

    gathers = []
    for step in range(1, group):
        copy = pltpu.make_async_remote_copy(
            src_ref=brick_ref.at[0],
            dst_ref=pencils.at[col_id, row_id],
            send_sem=sems1.at[0, step],
            recv_sem=sems1.at[1, step],
            device_id=brick_peer(step),
            device_id_type=MESH,
        )
        copy.start()
        gathers.append(copy)
    pencils[col_id, row_id] = brick_ref[0]
    energy[...] = jnp.zeros_like(energy)
    totals[...] = jnp.zeros_like(totals)
    tall[...] = jnp.zeros_like(tall)
    for copy in gathers:
        copy.wait_recv()

    both = None
    for part in range(bcols):
        term = dot(pencils[part].reshape(brows * rows, cols), forward_ref[part])
        both = term if both is None else both + term
    padded = both.shape[1] // 2
    real, imag = both[:, :padded], both[:, padded:]
    weights = lax.rsqrt(dot(real * real + imag * imag, smoothing_ref[...]) + epsilon)
    tall[half_edge : half_edge + brows * rows, :] = dot(
        real * weights, inverse_ref[col_id, :padded, :]
    ) + dot(imag * weights, inverse_ref[col_id, padded:, :])
    start = pl.multiple_of(row_id * rows, 8)
    windows[me] = tall[pl.ds(start, tile_rows), :]

    sends = []
    for step in range(1, orients):
        copy = pltpu.make_async_remote_copy(
            src_ref=windows.at[me],
            dst_ref=windows.at[me],
            send_sem=sems2.at[0, step],
            recv_sem=sems2.at[1, step],
            device_id=plane_peer(step),
            device_id_type=MESH,
        )
        copy.start()
        sends.append(copy)

    bunch = math.gcd(orients, 8)

    def absorb(plane):
        window = windows[plane]
        gap = plane - me
        near = jnp.logical_and(gap >= -half_edge, gap < half_edge).astype(jnp.float32)
        energy[...] += window * window * near
        transformed = dot(window, volume_dft_ref[...])
        spectrum[...] = transformed
        swapped[...] = pltpu.roll(transformed, transformed.shape[1] // 2, 1)

        def targets(piece):
            first = piece * bunch
            held = [totals[first + z] for z in range(bunch)]
            for b in range(edge):
                near_part = spectrum[b : b + rows, :]
                far_part = swapped[b : b + rows, :]
                for z in range(bunch):
                    a = plane - first - z + half_edge + lead
                    held[z] = held[z] + (
                        near_part * straight_ref[a, b : b + 1, :]
                        + far_part * crossed_ref[a, b : b + 1, :]
                    )
            for z in range(bunch):
                totals[first + z] = held[z]

        if orients == bunch:
            targets(0)
        else:
            pl.loop(0, orients // bunch)(targets)

    absorb(me)

    @pl.loop(1, orients)
    def _(step):
        source = lax.rem(me - step + orients, orients)
        pltpu.make_async_remote_copy(
            src_ref=windows.at[source],
            dst_ref=windows.at[source],
            send_sem=sems2.at[0, step],
            recv_sem=sems2.at[1, step],
            device_id=plane_peer(step),
            device_id_type=MESH,
        ).wait_recv()
        absorb(source)

    size = spectrum.shape[1]
    scored = dot(totals[...].reshape(orients * rows, size), score_dft_ref[...])
    scores[...] = scored.reshape(orients, rows, cols)
    returns = []
    for step in range(1, orients):
        copy = pltpu.make_async_remote_copy(
            src_ref=scores.at[lax.rem(me + step, orients)],
            dst_ref=arrived.at[step],
            send_sem=sems3.at[0, step],
            recv_sem=sems3.at[1, step],
            device_id=plane_peer(step),
            device_id_type=MESH,
        )
        copy.start()
        returns.append(copy)
    summed = energy[0:rows, :]
    for b in range(1, edge):
        summed = summed + energy[b : b + rows, :]
    scaling = lax.rsqrt(dot(summed, box_ref[...]) / voxels + epsilon)
    best = scores[me]
    for step, copy in zip(range(1, orients), returns):
        copy.wait_recv()
        best = jnp.maximum(best, arrived[step])
    best_ref[0] = best * scaling
    for copy in gathers + sends + returns:
        copy.wait_send()


def shards(volume, template, voxel_maps):
    orients, brows, bcols = (lax.axis_size(axis) for axis in ("orient", "brow", "bcol"))
    planes, rows, cols = volume.shape
    edge = template.shape[0]
    half_edge = edge // 2
    voxels = edge**3
    length = cols * bcols
    size = cols + edge
    tile_rows = rows + edge
    table_rows = round_up(voxels, LANES) // LANES
    table = jnp.pad(template.reshape(-1), (0, table_rows * LANES - voxels)).reshape(table_rows, LANES)
    width = round_up(edge * edge, LANES)
    index = jnp.pad(voxel_maps[0].reshape(edge * edge, edge).T, ((0, 0), (0, width - edge * edge)))
    lead = max(0, orients - 1 - half_edge)
    trail = max(0, half_edge + orients - edge)
    vmem = pl.BlockSpec(memory_space=pltpu.VMEM)
    spectra = jax.ShapeDtypeStruct((lead + edge + trail, edge, size), jnp.float32)
    straight, crossed = pl.pallas_call(
        lambda *refs: rotate_kernel(voxels, lead, *refs),
        out_shape=(spectra, spectra),
        in_specs=[vmem] * 3,
        out_specs=(vmem, vmem),
        scratch_shapes=[
            pltpu.VMEM((table_rows, LANES), jnp.float32),
            pltpu.VMEM((edge, width), jnp.float32),
        ],
        name="rotate",
    )(table, index, jnp.asarray(template_table(edge, size)))
    constants = (
        forward_table(length, bcols),
        smoothing_table(length),
        windowed_inverse(length, bcols, half_edge),
        volume_table(size),
        score_table(size, cols),
        box_table(size, cols, edge),
    )
    sizes = (orients, brows, bcols, edge, voxels, lead)
    return pl.pallas_call(
        lambda *refs: match_kernel(sizes, *refs),
        out_shape=jax.ShapeDtypeStruct((1, rows, cols), jnp.float32),
        in_specs=[vmem] * 9,
        out_specs=vmem,
        scratch_shapes=[
            pltpu.VMEM((bcols, brows, rows, cols), jnp.float32),
            pltpu.VMEM((brows * rows + edge, size), jnp.float32),
            pltpu.VMEM((orients, tile_rows, size), jnp.float32),
            pltpu.VMEM((tile_rows, size), jnp.float32),
            pltpu.VMEM((tile_rows, size), jnp.float32),
            pltpu.VMEM((tile_rows, size), jnp.float32),
            pltpu.VMEM((orients, rows, size), jnp.float32),
            pltpu.VMEM((orients, rows, cols), jnp.float32),
            pltpu.VMEM((orients, rows, cols), jnp.float32),
            pltpu.SemaphoreType.DMA((2, brows * bcols)),
            pltpu.SemaphoreType.DMA((2, orients)),
            pltpu.SemaphoreType.DMA((2, orients)),
        ],
        compiler_params=pltpu.CompilerParams(collective_id=0, has_side_effects=True),
        name="match",
    )(volume, straight, crossed, *(jnp.asarray(c) for c in constants))


def solution(mesh):
    in_specs = (P("orient", "brow", "bcol"), P(), P("orient", None))
    out_specs = P("orient", "brow", "bcol")
    return jax.shard_map(shards, mesh=mesh, in_specs=in_specs, out_specs=out_specs, check_vma=False)
```

```python
import math

import numpy as np
import jax
import jax.numpy as jnp
from jax import lax
from jax.experimental import pallas as pl
from jax.experimental.pallas import tpu as pltpu
from jax.sharding import PartitionSpec as P

epsilon = 1e-06
floor_share = 0.1
highest = lax.Precision.HIGHEST
LANES = 128
MESH = pl.DeviceIdType.MESH


def round_up(value, step):
    return -(-value // step) * step


def forward_table(length, parts):
    half = length // 2 + 1
    padded = round_up(half, LANES)
    angles = 2.0 * np.pi * (np.outer(np.arange(length), np.arange(half)) % length) / length
    table = np.zeros((length, 2 * padded))
    table[:, :half] = np.cos(angles)
    table[:, padded : padded + half] = -np.sin(angles)
    return table.reshape(parts, length // parts, 2 * padded).astype(np.float32)


def smoothing_table(length):
    half = length // 2 + 1
    padded = round_up(half, LANES)
    table = np.zeros((padded, padded))
    fold = np.minimum(np.arange(length), length - np.arange(length))
    for k in range(half):
        for shift in (-1, 0, 1):
            table[fold[(k + shift) % length], k] += 1.0 / 3.0
        for other in range(length):
            table[fold[other], k] += floor_share / length
    return table.astype(np.float32)


def windowed_inverse(length, parts, margin):
    half = length // 2 + 1
    padded = round_up(half, LANES)
    width = length // parts
    tables = np.zeros((parts, 2 * padded, width + 2 * margin))
    k = np.arange(half)
    share = np.where((k == 0) | (2 * k == length), 1.0, 2.0)[:, None] / math.sqrt(length)
    for part in range(parts):
        columns = np.arange(width + 2 * margin) + part * width - margin
        inside = (columns >= 0) & (columns < length)
        angles = 2.0 * np.pi * (np.outer(k, columns) % length) / length
        tables[part, :half] = share * np.cos(angles) * inside
        tables[part, padded : padded + half] = -share * np.sin(angles) * inside
    return tables.astype(np.float32)


def packed_dft(count, size):
    k = np.arange(size)
    real = k <= size // 2
    freq = np.where(real, k, k - size // 2)
    angles = 2.0 * np.pi * (np.outer(np.arange(count), freq) % size) / size
    return angles, real, freq


def volume_table(size):
    angles, real, freq = packed_dft(size, size)
    return np.where(real, np.cos(angles), -np.sin(angles)).astype(np.float32)


def template_table(count, size):
    angles, real, freq = packed_dft(count, size)
    straight = np.cos(angles)
    edge = (freq == 0) | (freq == size // 2)
    crossed = np.where(real, -np.sin(angles), np.sin(angles)) * ~edge
    return np.concatenate([straight, crossed], axis=1).astype(np.float32)


def score_table(size, count):
    angles, real, freq = packed_dft(count, size)
    share = np.where((freq == 0) | (freq == size // 2), 1.0, 2.0)
    return (np.where(real, np.cos(angles), -np.sin(angles)) * share / size).T.astype(np.float32)


def box_table(size, count, edge):
    offsets = np.arange(size)[:, None] - np.arange(count)[None, :]
    return ((offsets >= 0) & (offsets < edge)).astype(np.float32)


def dot(a, b):
    return jnp.dot(a, b, precision=highest, preferred_element_type=jnp.float32)


def split_table(template_ref, normed):
    lines, edge = template_ref.shape
    template = template_ref[...]
    centred = template - jnp.sum(template, keepdims=True) / (lines * edge)
    normed[...] = centred / jnp.sqrt(jnp.sum(centred * centred, keepdims=True) + epsilon)
    table = jnp.concatenate([normed[pl.ds(j, lines // 8, stride=8), :] for j in range(8)], axis=1)
    spare = round_up(lines // 8, 16) - lines // 8
    table = jnp.concatenate([table, jnp.zeros((spare, 8 * edge), jnp.float32)], axis=0)
    upper = table.astype(jnp.bfloat16)
    lower = (table - upper.astype(jnp.float32)).astype(jnp.bfloat16)
    return jnp.concatenate([upper, lower], axis=0)


def look_up(pieces, index):
    count, span = pieces.shape
    width = index.shape[1]
    high = ((index.astype(jnp.float32) + 0.5) * (1.0 / span)).astype(jnp.int32)
    low = index - high * span
    chosen = lax.broadcasted_iota(jnp.int32, (span, width), 0) == low
    lanes = jnp.dot(
        pieces,
        jnp.where(chosen, 1.0, 0.0).astype(jnp.bfloat16),
        preferred_element_type=jnp.float32,
    )
    lanes = lanes[: count // 2] + lanes[count // 2 :]
    mine = lax.broadcasted_iota(jnp.int32, lanes.shape, 0) == high
    return jnp.sum(jnp.where(mine, lanes, 0.0), axis=0, keepdims=True)


def match_kernel(
    sizes,
    brick_ref,
    template_ref,
    index_ref,
    template_dft_ref,
    forward_ref,
    smoothing_ref,
    inverse_ref,
    volume_dft_ref,
    score_dft_ref,
    box_ref,
    best_ref,
    scaling_ref,
    normed,
    rotated,
    straight_ref,
    crossed_ref,
    pencils,
    tall,
    windows,
    spectrum,
    swapped,
    energy,
    totals,
    scores,
    arrived,
    sems0,
    sems1,
    sems2,
    sems3,
):
    orients, brows, bcols, edge, voxels, lead, taken = sizes
    half_edge = edge // 2
    rows, cols = brick_ref.shape[1:]
    tile_rows = windows.shape[1]
    me = lax.axis_index("orient")
    row_id = lax.axis_index("brow")
    col_id = lax.axis_index("bcol")
    group = brows * bcols
    place = row_id * bcols + col_id

    def brick_peer(step):
        other = lax.rem(place + step, group)
        return {"orient": me, "brow": other // bcols, "bcol": lax.rem(other, bcols)}

    def plane_peer(step):
        return {"orient": lax.rem(me + step, orients), "brow": row_id, "bcol": col_id}

    windows[...] = jnp.zeros_like(windows)
    barrier = pltpu.get_barrier_semaphore()
    for step in range(1, group):
        pl.semaphore_signal(barrier, inc=1, device_id=brick_peer(step), device_id_type=MESH)
    for step in range(1, orients):
        pl.semaphore_signal(barrier, inc=1, device_id=plane_peer(step), device_id_type=MESH)

    energy[...] = jnp.zeros_like(energy)
    totals[...] = jnp.zeros_like(totals)
    tall[...] = jnp.zeros_like(tall)
    rotated[place] = jnp.zeros(rotated.shape[1:], jnp.float32)
    share = index_ref.shape[1]
    pieces = split_table(template_ref, normed)
    for i in range(share):
        rotated[place, i : i + 1, :] = look_up(pieces, index_ref[place, i : i + 1, :])

    pl.semaphore_wait(barrier, group + orients - 2)

    gathers = []
    for step in range(1, group):
        copy = pltpu.make_async_remote_copy(
            src_ref=brick_ref.at[0],
            dst_ref=pencils.at[col_id, row_id],
            send_sem=sems1.at[0, step],
            recv_sem=sems1.at[1, step],
            device_id=brick_peer(step),
            device_id_type=MESH,
        )
        copy.start()
        gathers.append(copy)
    shares = []
    for step in range(1, group):
        copy = pltpu.make_async_remote_copy(
            src_ref=rotated.at[place],
            dst_ref=rotated.at[place],
            send_sem=sems0.at[0, step],
            recv_sem=sems0.at[1, step],
            device_id=brick_peer(step),
            device_id_type=MESH,
        )
        copy.start()
        shares.append(copy)
    pencils[col_id, row_id] = brick_ref[0]
    for copy in gathers:
        copy.wait_recv()

    both = None
    for part in range(bcols):
        term = dot(pencils[part].reshape(brows * rows, cols), forward_ref[part])
        both = term if both is None else both + term
    padded = both.shape[1] // 2
    real, imag = both[:, :padded], both[:, padded:]
    weights = lax.rsqrt(dot(real * real + imag * imag, smoothing_ref[...]) + epsilon)
    tall[half_edge : half_edge + brows * rows, :] = dot(
        real * weights, inverse_ref[col_id, :padded, :]
    ) + dot(imag * weights, inverse_ref[col_id, padded:, :])
    start = pl.multiple_of(row_id * rows, 8)
    windows[me] = tall[pl.ds(start, tile_rows), :]
    idle = half_edge // 8 * 8 if brows == 2 else 0
    filled = pl.ds(pl.multiple_of((brows - 1 - row_id) * idle, 8), tile_rows - idle)

    sends = []
    for step in range(1, orients):
        copy = pltpu.make_async_remote_copy(
            src_ref=windows.at[me, filled],
            dst_ref=windows.at[me, filled],
            send_sem=sems2.at[0, step],
            recv_sem=sems2.at[1, step],
            device_id=plane_peer(step),
            device_id_type=MESH,
        )
        copy.start()
        sends.append(copy)

    for copy in shares:
        copy.wait_recv()
    turned = None
    for part in range(group):
        term = lax.dot_general(
            rotated[part],
            template_dft_ref[part],
            (((0,), (0,)), ((), ())),
            precision=highest,
            preferred_element_type=jnp.float32,
        )
        turned = term if turned is None else turned + term
    size = turned.shape[1] // 2
    if straight_ref.shape[0] > taken:
        straight_ref[...] = jnp.zeros_like(straight_ref)
        crossed_ref[...] = jnp.zeros_like(crossed_ref)
    straight_ref[lead : lead + taken] = turned[:, :size].reshape(taken, edge, size)
    crossed_ref[lead : lead + taken] = turned[:, size:].reshape(taken, edge, size)

    bunch = math.gcd(orients, 8)

    def absorb(plane):
        window = windows[plane]
        gap = plane - me
        near = jnp.logical_and(gap >= -half_edge, gap < half_edge).astype(jnp.float32)
        energy[...] += window * window * near
        transformed = dot(window, volume_dft_ref[...])
        spectrum[...] = transformed
        swapped[...] = pltpu.roll(transformed, transformed.shape[1] // 2, 1)

        def targets(piece):
            first = piece * bunch
            held = [totals[first + z] for z in range(bunch)]
            for b in range(edge):
                near_part = spectrum[b : b + rows, :]
                far_part = swapped[b : b + rows, :]
                for z in range(bunch):
                    a = plane - first - z + orients - 1
                    held[z] = held[z] + (
                        near_part * straight_ref[a, b : b + 1, :]
                        + far_part * crossed_ref[a, b : b + 1, :]
                    )
            for z in range(bunch):
                totals[first + z] = held[z]

        if orients == bunch:
            targets(0)
        else:
            pl.loop(0, orients // bunch)(targets)

    absorb(me)

    @pl.loop(1, orients)
    def _(step):
        source = lax.rem(me - step + orients, orients)
        pltpu.make_async_remote_copy(
            src_ref=windows.at[source, filled],
            dst_ref=windows.at[source, filled],
            send_sem=sems2.at[0, step],
            recv_sem=sems2.at[1, step],
            device_id=plane_peer(step),
            device_id_type=MESH,
        ).wait_recv()
        absorb(source)

    scored = dot(totals[...].reshape(orients * rows, size), score_dft_ref[...])
    scores[...] = scored.reshape(orients, rows, cols)
    returns = []
    for step in range(1, orients):
        copy = pltpu.make_async_remote_copy(
            src_ref=scores.at[lax.rem(me + step, orients)],
            dst_ref=arrived.at[step],
            send_sem=sems3.at[0, step],
            recv_sem=sems3.at[1, step],
            device_id=plane_peer(step),
            device_id_type=MESH,
        )
        copy.start()
        returns.append(copy)
    summed = energy[0:rows, :]
    for b in range(1, edge):
        summed = summed + energy[b : b + rows, :]
    scaling = lax.rsqrt(dot(summed, box_ref[...]) / voxels + epsilon)
    best = scores[me]
    for step, copy in zip(range(1, orients), returns):
        copy.wait_recv()
        best = jnp.maximum(best, arrived[step])
    best_ref[0] = best
    scaling_ref[0] = scaling
    for copy in gathers + shares + sends + returns:
        copy.wait_send()


def shards(volume, template, voxel_maps):
    orients, brows, bcols = (lax.axis_size(axis) for axis in ("orient", "brow", "bcol"))
    planes, rows, cols = volume.shape
    edge = template.shape[0]
    half_edge = edge // 2
    voxels = edge**3
    length = cols * bcols
    size = cols + edge
    tile_rows = rows + edge
    group = brows * bcols
    share = -(-edge // group)
    first = max(0, half_edge - orients + 1)
    taken = min(edge, half_edge + orients) - first
    lead = first - (half_edge - orients + 1)
    index = voxel_maps.reshape(edge, edge, edge)[first : first + taken].reshape(taken * edge, edge).T
    index = jnp.pad(index, ((0, share * group - edge), (0, 0))).reshape(group, share, taken * edge)
    held = round_up(share, 8)
    template_dft = np.zeros((group, held, 2 * size), np.float32)
    for c, line in enumerate(template_table(edge, size)):
        template_dft[c // share, c % share] = line
    vmem = pl.BlockSpec(memory_space=pltpu.VMEM)
    constants = (
        template_dft,
        forward_table(length, bcols),
        smoothing_table(length),
        windowed_inverse(length, bcols, half_edge),
        volume_table(size),
        score_table(size, cols),
        box_table(size, cols, edge),
    )
    sizes = (orients, brows, bcols, edge, voxels, lead, taken)
    best, scaling = pl.pallas_call(
        lambda *refs: match_kernel(sizes, *refs),
        out_shape=(jax.ShapeDtypeStruct((1, rows, cols), jnp.float32),) * 2,
        in_specs=[vmem] * 10,
        out_specs=(vmem, vmem),
        scratch_shapes=[
            pltpu.VMEM((edge * edge, edge), jnp.float32),
            pltpu.VMEM((group, held, taken * edge), jnp.float32),
            pltpu.VMEM((2 * orients - 1, edge, size), jnp.float32),
            pltpu.VMEM((2 * orients - 1, edge, size), jnp.float32),
            pltpu.VMEM((bcols, brows, rows, cols), jnp.float32),
            pltpu.VMEM((brows * rows + edge, size), jnp.float32),
            pltpu.VMEM((orients, tile_rows, size), jnp.float32),
            pltpu.VMEM((tile_rows, size), jnp.float32),
            pltpu.VMEM((tile_rows, size), jnp.float32),
            pltpu.VMEM((tile_rows, size), jnp.float32),
            pltpu.VMEM((orients, rows, size), jnp.float32),
            pltpu.VMEM((orients, rows, cols), jnp.float32),
            pltpu.VMEM((orients, rows, cols), jnp.float32),
            pltpu.SemaphoreType.DMA((2, group)),
            pltpu.SemaphoreType.DMA((2, group)),
            pltpu.SemaphoreType.DMA((2, orients)),
            pltpu.SemaphoreType.DMA((2, orients)),
        ],
        compiler_params=pltpu.CompilerParams(collective_id=0, has_side_effects=True),
        name="match",
    )(volume, template.reshape(edge * edge, edge), index, *(jnp.asarray(c) for c in constants))
    return best * scaling


def solution(mesh):
    in_specs = (P("orient", "brow", "bcol"), P(), P("orient", None))
    out_specs = P("orient", "brow", "bcol")
    return jax.shard_map(shards, mesh=mesh, in_specs=in_specs, out_specs=out_specs, check_vma=False)
```

```python
import math

import numpy as np
import jax
import jax.numpy as jnp
from jax import lax
from jax.experimental import pallas as pl
from jax.experimental.pallas import tpu as pltpu
from jax.sharding import PartitionSpec as P

epsilon = 1e-06
floor_share = 0.1
highest = lax.Precision.HIGHEST
LANES = 128
MESH = pl.DeviceIdType.MESH


def round_up(value, step):
    return -(-value // step) * step


def forward_table(length, parts):
    half = length // 2 + 1
    padded = round_up(half, LANES)
    angles = 2.0 * np.pi * (np.outer(np.arange(length), np.arange(half)) % length) / length
    table = np.zeros((length, 2 * padded))
    table[:, :half] = np.cos(angles)
    table[:, padded : padded + half] = -np.sin(angles)
    return table.reshape(parts, length // parts, 2 * padded).astype(np.float32)


def smoothing_table(length):
    half = length // 2 + 1
    padded = round_up(half, LANES)
    table = np.zeros((padded, padded))
    fold = np.minimum(np.arange(length), length - np.arange(length))
    for k in range(half):
        for shift in (-1, 0, 1):
            table[fold[(k + shift) % length], k] += 1.0 / 3.0
        for other in range(length):
            table[fold[other], k] += floor_share / length
    return table.astype(np.float32)


def windowed_inverse(length, parts, margin):
    half = length // 2 + 1
    padded = round_up(half, LANES)
    width = length // parts
    tables = np.zeros((parts, 2 * padded, width + 2 * margin))
    k = np.arange(half)
    share = np.where((k == 0) | (2 * k == length), 1.0, 2.0)[:, None] / math.sqrt(length)
    for part in range(parts):
        columns = np.arange(width + 2 * margin) + part * width - margin
        inside = (columns >= 0) & (columns < length)
        angles = 2.0 * np.pi * (np.outer(k, columns) % length) / length
        tables[part, :half] = share * np.cos(angles) * inside
        tables[part, padded : padded + half] = -share * np.sin(angles) * inside
    return tables.astype(np.float32)


def packed_dft(count, size):
    k = np.arange(size)
    real = k <= size // 2
    freq = np.where(real, k, k - size // 2)
    angles = 2.0 * np.pi * (np.outer(np.arange(count), freq) % size) / size
    return angles, real, freq


def volume_table(size):
    angles, real, freq = packed_dft(size, size)
    return np.where(real, np.cos(angles), -np.sin(angles)).astype(np.float32)


def template_table(count, size):
    angles, real, freq = packed_dft(count, size)
    straight = np.cos(angles)
    edge = (freq == 0) | (freq == size // 2)
    crossed = np.where(real, -np.sin(angles), np.sin(angles)) * ~edge
    return np.concatenate([straight, crossed], axis=1).astype(np.float32)


def score_table(size, count):
    angles, real, freq = packed_dft(count, size)
    share = np.where((freq == 0) | (freq == size // 2), 1.0, 2.0)
    return (np.where(real, np.cos(angles), -np.sin(angles)) * share / size).T.astype(np.float32)


def box_table(size, count, edge):
    offsets = np.arange(size)[:, None] - np.arange(count)[None, :]
    return ((offsets >= 0) & (offsets < edge)).astype(np.float32)


def dot(a, b):
    return jnp.dot(a, b, precision=highest, preferred_element_type=jnp.float32)


def split_table(template_ref, normed):
    lines, edge = template_ref.shape
    template = template_ref[...]
    centred = template - jnp.sum(template, keepdims=True) / (lines * edge)
    normed[...] = centred / jnp.sqrt(jnp.sum(centred * centred, keepdims=True) + epsilon)
    table = jnp.concatenate([normed[pl.ds(j, lines // 8, stride=8), :] for j in range(8)], axis=1)
    spare = round_up(lines // 8, 16) - lines // 8
    table = jnp.concatenate([table, jnp.zeros((spare, 8 * edge), jnp.float32)], axis=0)
    upper = table.astype(jnp.bfloat16)
    lower = (table - upper.astype(jnp.float32)).astype(jnp.bfloat16)
    return jnp.concatenate([upper, lower], axis=0)


def look_up(pieces, index):
    count, span = pieces.shape
    width = index.shape[1]
    high = ((index.astype(jnp.float32) + 0.5) * (1.0 / span)).astype(jnp.int32)
    low = index - high * span
    chosen = lax.broadcasted_iota(jnp.int32, (span, width), 0) == low
    lanes = jnp.dot(
        pieces,
        jnp.where(chosen, 1.0, 0.0).astype(jnp.bfloat16),
        preferred_element_type=jnp.float32,
    )
    lanes = lanes[: count // 2] + lanes[count // 2 :]
    mine = lax.broadcasted_iota(jnp.int32, lanes.shape, 0) == high
    return jnp.sum(jnp.where(mine, lanes, 0.0), axis=0, keepdims=True)


def match_kernel(
    sizes,
    brick_ref,
    template_ref,
    index_ref,
    template_dft_ref,
    forward_ref,
    smoothing_ref,
    inverse_ref,
    volume_dft_ref,
    score_dft_ref,
    box_ref,
    best_ref,
    scaling_ref,
    normed,
    rotated,
    rotations,
    straight_ref,
    crossed_ref,
    pencils,
    tall,
    windows,
    spectrum,
    swapped,
    energy,
    totals,
    sems0,
    sems1,
    sems2,
):
    orients, brows, bcols, edge, voxels, base, first, last = sizes
    half_edge = edge // 2
    rows, cols = brick_ref.shape[1:]
    tile_rows = windows.shape[1]
    me = lax.axis_index("orient")
    row_id = lax.axis_index("brow")
    col_id = lax.axis_index("bcol")
    group = brows * bcols
    place = row_id * bcols + col_id

    def brick_peer(step):
        other = lax.rem(place + step, group)
        return {"orient": me, "brow": other // bcols, "bcol": lax.rem(other, bcols)}

    def plane_peer(step):
        return {"orient": lax.rem(me + step, orients), "brow": row_id, "bcol": col_id}

    windows[...] = jnp.zeros_like(windows)
    barrier = pltpu.get_barrier_semaphore()
    for step in range(1, group):
        pl.semaphore_signal(barrier, inc=1, device_id=brick_peer(step), device_id_type=MESH)
    for step in range(1, orients):
        pl.semaphore_signal(barrier, inc=1, device_id=plane_peer(step), device_id_type=MESH)

    energy[...] = jnp.zeros_like(energy)
    totals[...] = jnp.zeros_like(totals)
    tall[...] = jnp.zeros_like(tall)
    if first > base or last < base + rotated.shape[0]:
        rotated[...] = jnp.zeros_like(rotated)
    pieces = split_table(template_ref, normed)

    pl.semaphore_wait(barrier, group + orients - 2)

    gathers = []
    for step in range(1, group):
        copy = pltpu.make_async_remote_copy(
            src_ref=brick_ref.at[0],
            dst_ref=pencils.at[col_id, row_id],
            send_sem=sems1.at[0, step],
            recv_sem=sems1.at[1, step],
            device_id=brick_peer(step),
            device_id_type=MESH,
        )
        copy.start()
        gathers.append(copy)
    pencils[col_id, row_id] = brick_ref[0]
    plane_voxels = edge * edge

    @pl.loop(0, (last - first) // 2)
    def _(pair):
        start = pl.multiple_of((first + 2 * pair) * plane_voxels, 2 * plane_voxels)
        found = look_up(pieces, index_ref[0:1, pl.ds(start, 2 * plane_voxels)])
        for i in range(2):
            rotated[first - base + 2 * pair + i] = found[:, i * plane_voxels : (i + 1) * plane_voxels]

    shares = []
    for step in range(1, orients):
        target = lax.rem(me + step, orients)
        copy = pltpu.make_async_remote_copy(
            src_ref=rotated.at[pl.ds(half_edge - target - base, orients)],
            dst_ref=rotations.at[me],
            send_sem=sems0.at[0, step],
            recv_sem=sems0.at[1, step],
            device_id=plane_peer(step),
            device_id_type=MESH,
        )
        copy.start()
        shares.append(copy)
    rotations[me] = rotated[pl.ds(half_edge - me - base, orients)]
    for copy in gathers:
        copy.wait_recv()

    both = None
    for part in range(bcols):
        term = dot(pencils[part].reshape(brows * rows, cols), forward_ref[part])
        both = term if both is None else both + term
    padded = both.shape[1] // 2
    real, imag = both[:, :padded], both[:, padded:]
    weights = lax.rsqrt(dot(real * real + imag * imag, smoothing_ref[...]) + epsilon)
    tall[half_edge : half_edge + brows * rows, :] = dot(
        real * weights, inverse_ref[col_id, :padded, :]
    ) + dot(imag * weights, inverse_ref[col_id, padded:, :])
    start = pl.multiple_of(row_id * rows, 8)
    windows[me] = tall[pl.ds(start, tile_rows), :]
    idle = half_edge // 8 * 8 if brows == 2 else 0
    filled = pl.ds(pl.multiple_of((brows - 1 - row_id) * idle, 8), tile_rows - idle)

    sends = []
    for step in range(1, orients):
        copy = pltpu.make_async_remote_copy(
            src_ref=windows.at[me, filled],
            dst_ref=windows.at[me, filled],
            send_sem=sems2.at[0, step],
            recv_sem=sems2.at[1, step],
            device_id=plane_peer(step),
            device_id_type=MESH,
        )
        copy.start()
        sends.append(copy)

    def unfold(rotation):
        planes = rotations[rotation][:, 0, :]
        lines = jnp.concatenate(
            [planes[:, b * edge : (b + 1) * edge] for b in range(edge)], axis=0
        )
        turned = dot(lines, template_dft_ref[...])
        size = turned.shape[1] // 2
        straight_ref[rotation] = turned[:, :size].reshape(edge, orients, size)
        crossed_ref[rotation] = turned[:, size:].reshape(edge, orients, size)

    unfold(me)

    @pl.loop(1, orients)
    def _(step):
        source = lax.rem(me - step + orients, orients)
        pltpu.make_async_remote_copy(
            src_ref=rotated.at[pl.ds(half_edge - me - base, orients)],
            dst_ref=rotations.at[source],
            send_sem=sems0.at[0, step],
            recv_sem=sems0.at[1, step],
            device_id=plane_peer(step),
            device_id_type=MESH,
        ).wait_recv()
        unfold(source)

    bunch = math.gcd(orients, 8)

    def absorb(plane):
        window = windows[plane]
        gap = plane - me
        near = jnp.logical_and(gap >= -half_edge, gap < half_edge).astype(jnp.float32)
        energy[...] += window * window * near
        transformed = dot(window, volume_dft_ref[...])
        spectrum[...] = transformed
        swapped[...] = pltpu.roll(transformed, transformed.shape[1] // 2, 1)

        def targets(piece):
            lowest = piece * bunch
            held = [totals[lowest + r] for r in range(bunch)]
            for b in range(edge):
                near_part = spectrum[b : b + rows, :]
                far_part = swapped[b : b + rows, :]
                for r in range(bunch):
                    held[r] = held[r] + (
                        near_part * straight_ref[lowest + r, b, pl.ds(plane, 1), :]
                        + far_part * crossed_ref[lowest + r, b, pl.ds(plane, 1), :]
                    )
            for r in range(bunch):
                totals[lowest + r] = held[r]

        if orients == bunch:
            targets(0)
        else:
            pl.loop(0, orients // bunch)(targets)

    absorb(me)

    @pl.loop(1, orients)
    def _(step):
        source = lax.rem(me - step + orients, orients)
        pltpu.make_async_remote_copy(
            src_ref=windows.at[source, filled],
            dst_ref=windows.at[source, filled],
            send_sem=sems2.at[0, step],
            recv_sem=sems2.at[1, step],
            device_id=plane_peer(step),
            device_id_type=MESH,
        ).wait_recv()
        absorb(source)

    summed = energy[0:rows, :]
    for b in range(1, edge):
        summed = summed + energy[b : b + rows, :]
    scaling = lax.rsqrt(dot(summed, box_ref[...]) / voxels + epsilon)
    size = spectrum.shape[1]
    scored = dot(totals[...].reshape(orients * rows, size), score_dft_ref[...])
    best = jnp.max(scored.reshape(orients, rows, cols), axis=0)
    best_ref[0] = best
    scaling_ref[0] = scaling
    for copy in gathers + shares + sends:
        copy.wait_send()


def shards(volume, template, voxel_maps):
    orients, brows, bcols = (lax.axis_size(axis) for axis in ("orient", "brow", "bcol"))
    planes, rows, cols = volume.shape
    edge = template.shape[0]
    half_edge = edge // 2
    voxels = edge**3
    length = cols * bcols
    size = cols + edge
    tile_rows = rows + edge
    base = (half_edge - orients + 1) // 2 * 2
    first = max(0, base)
    last = min(edge, round_up(half_edge + orients, 2))
    held = round_up(half_edge + orients, 2) - base
    group = brows * bcols
    vmem = pl.BlockSpec(memory_space=pltpu.VMEM)
    constants = (
        template_table(edge, size),
        forward_table(length, bcols),
        smoothing_table(length),
        windowed_inverse(length, bcols, half_edge),
        volume_table(size),
        score_table(size, cols),
        box_table(size, cols, edge),
    )
    sizes = (orients, brows, bcols, edge, voxels, base, first, last)
    best, scaling = pl.pallas_call(
        lambda *refs: match_kernel(sizes, *refs),
        out_shape=(jax.ShapeDtypeStruct((1, rows, cols), jnp.float32),) * 2,
        in_specs=[vmem] * 10,
        out_specs=(vmem, vmem),
        scratch_shapes=[
            pltpu.VMEM((edge * edge, edge), jnp.float32),
            pltpu.VMEM((held, 1, edge * edge), jnp.float32),
            pltpu.VMEM((orients, orients, 1, edge * edge), jnp.float32),
            pltpu.VMEM((orients, edge, orients, size), jnp.float32),
            pltpu.VMEM((orients, edge, orients, size), jnp.float32),
            pltpu.VMEM((bcols, brows, rows, cols), jnp.float32),
            pltpu.VMEM((brows * rows + edge, size), jnp.float32),
            pltpu.VMEM((orients, tile_rows, size), jnp.float32),
            pltpu.VMEM((tile_rows, size), jnp.float32),
            pltpu.VMEM((tile_rows, size), jnp.float32),
            pltpu.VMEM((tile_rows, size), jnp.float32),
            pltpu.VMEM((orients, rows, size), jnp.float32),
            pltpu.SemaphoreType.DMA((2, orients)),
            pltpu.SemaphoreType.DMA((2, group)),
            pltpu.SemaphoreType.DMA((2, orients)),
        ],
        compiler_params=pltpu.CompilerParams(collective_id=0, has_side_effects=True),
        name="match",
    )(volume, template.reshape(edge * edge, edge), voxel_maps, *(jnp.asarray(c) for c in constants))
    return best * scaling


def solution(mesh):
    in_specs = (P("orient", "brow", "bcol"), P(), P("orient", None))
    out_specs = P("orient", "brow", "bcol")
    return jax.shard_map(shards, mesh=mesh, in_specs=in_specs, out_specs=out_specs, check_vma=False)
```

```python
import math

import numpy as np
import jax
import jax.numpy as jnp
from jax import lax
from jax.experimental import pallas as pl
from jax.experimental.pallas import tpu as pltpu
from jax.sharding import PartitionSpec as P

epsilon = 1e-06
floor_share = 0.1
highest = lax.Precision.HIGHEST
LANES = 128
MESH = pl.DeviceIdType.MESH


def round_up(value, step):
    return -(-value // step) * step


def forward_table(length, parts):
    half = length // 2 + 1
    padded = round_up(half, LANES)
    angles = 2.0 * np.pi * (np.outer(np.arange(length), np.arange(half)) % length) / length
    table = np.zeros((length, 2 * padded))
    table[:, :half] = np.cos(angles)
    table[:, padded : padded + half] = -np.sin(angles)
    return table.reshape(parts, length // parts, 2 * padded).astype(np.float32)


def smoothing_table(length):
    half = length // 2 + 1
    padded = round_up(half, LANES)
    table = np.zeros((padded, padded))
    fold = np.minimum(np.arange(length), length - np.arange(length))
    for k in range(half):
        for shift in (-1, 0, 1):
            table[fold[(k + shift) % length], k] += 1.0 / 3.0
        for other in range(length):
            table[fold[other], k] += floor_share / length
    return table.astype(np.float32)


def windowed_inverse(length, parts, margin):
    half = length // 2 + 1
    padded = round_up(half, LANES)
    width = length // parts
    tables = np.zeros((parts, 2 * padded, width + 2 * margin))
    k = np.arange(half)
    share = np.where((k == 0) | (2 * k == length), 1.0, 2.0)[:, None] / math.sqrt(length)
    for part in range(parts):
        columns = np.arange(width + 2 * margin) + part * width - margin
        inside = (columns >= 0) & (columns < length)
        angles = 2.0 * np.pi * (np.outer(k, columns) % length) / length
        tables[part, :half] = share * np.cos(angles) * inside
        tables[part, padded : padded + half] = -share * np.sin(angles) * inside
    return tables.astype(np.float32)


def packed_dft(count, size):
    k = np.arange(size)
    real = k <= size // 2
    freq = np.where(real, k, k - size // 2)
    angles = 2.0 * np.pi * (np.outer(np.arange(count), freq) % size) / size
    return angles, real, freq


def volume_table(size):
    angles, real, freq = packed_dft(size, size)
    return np.where(real, np.cos(angles), -np.sin(angles)).astype(np.float32)


def template_table(count, size):
    angles, real, freq = packed_dft(count, size)
    straight = np.cos(angles)
    edge = (freq == 0) | (freq == size // 2)
    crossed = np.where(real, -np.sin(angles), np.sin(angles)) * ~edge
    return np.concatenate([straight, crossed], axis=1).astype(np.float32)


def score_table(size, count):
    angles, real, freq = packed_dft(count, size)
    share = np.where((freq == 0) | (freq == size // 2), 1.0, 2.0)
    return (np.where(real, np.cos(angles), -np.sin(angles)) * share / size).T.astype(np.float32)


def box_table(size, count, edge):
    offsets = np.arange(size)[:, None] - np.arange(count)[None, :]
    return ((offsets >= 0) & (offsets < edge)).astype(np.float32)


def dot(a, b):
    return jnp.dot(a, b, precision=highest, preferred_element_type=jnp.float32)


def split_table(template_ref, normed):
    lines, edge = template_ref.shape
    template = template_ref[...]
    centred = template - jnp.sum(template, keepdims=True) / (lines * edge)
    normed[...] = centred / jnp.sqrt(jnp.sum(centred * centred, keepdims=True) + epsilon)
    table = jnp.concatenate([normed[pl.ds(j, lines // 8, stride=8), :] for j in range(8)], axis=1)
    spare = round_up(lines // 8, 16) - lines // 8
    table = jnp.concatenate([table, jnp.zeros((spare, 8 * edge), jnp.float32)], axis=0)
    upper = table.astype(jnp.bfloat16)
    lower = (table - upper.astype(jnp.float32)).astype(jnp.bfloat16)
    return jnp.concatenate([upper, lower], axis=0)


def look_up(pieces, index):
    count, span = pieces.shape
    width = index.shape[1]
    high = ((index.astype(jnp.float32) + 0.5) * (1.0 / span)).astype(jnp.int32)
    low = index - high * span
    chosen = lax.broadcasted_iota(jnp.int32, (span, width), 0) == low
    lanes = jnp.dot(
        pieces,
        jnp.where(chosen, 1.0, 0.0).astype(jnp.bfloat16),
        preferred_element_type=jnp.float32,
    )
    lanes = lanes[: count // 2] + lanes[count // 2 :]
    mine = lax.broadcasted_iota(jnp.int32, lanes.shape, 0) == high
    return jnp.sum(jnp.where(mine, lanes, 0.0), axis=0, keepdims=True)


def match_kernel(
    sizes,
    brick_ref,
    template_ref,
    index_ref,
    template_dft_ref,
    forward_ref,
    smoothing_ref,
    inverse_ref,
    volume_dft_ref,
    score_dft_ref,
    box_ref,
    best_ref,
    scaling_ref,
    normed,
    rotated,
    rotations,
    straight_ref,
    crossed_ref,
    pencils,
    tall,
    windows,
    spectrum,
    swapped,
    energy,
    totals,
    sems0,
    sems1,
    sems2,
):
    orients, brows, bcols, edge, voxels, base, first, last = sizes
    half_edge = edge // 2
    rows, cols = brick_ref.shape[1:]
    tile_rows = windows.shape[1]
    me = lax.axis_index("orient")
    row_id = lax.axis_index("brow")
    col_id = lax.axis_index("bcol")
    group = brows * bcols
    place = row_id * bcols + col_id

    def brick_peer(step):
        other = lax.rem(place + step, group)
        return {"orient": me, "brow": other // bcols, "bcol": lax.rem(other, bcols)}

    def plane_peer(step):
        return {"orient": lax.rem(me + step, orients), "brow": row_id, "bcol": col_id}

    windows[...] = jnp.zeros_like(windows)
    barrier = pltpu.get_barrier_semaphore()
    for step in range(1, group):
        pl.semaphore_signal(barrier, inc=1, device_id=brick_peer(step), device_id_type=MESH)
    for step in range(1, orients):
        pl.semaphore_signal(barrier, inc=1, device_id=plane_peer(step), device_id_type=MESH)

    energy[...] = jnp.zeros_like(energy)
    totals[...] = jnp.zeros_like(totals)
    tall[...] = jnp.zeros_like(tall)
    if first > base or last < base + rotated.shape[0]:
        rotated[...] = jnp.zeros_like(rotated)
    pieces = split_table(template_ref, normed)

    plane_voxels = edge * edge

    @pl.loop(0, (last - first) // 2)
    def _(pair):
        start = pl.multiple_of((first + 2 * pair) * plane_voxels, 2 * plane_voxels)
        found = look_up(pieces, index_ref[0:1, pl.ds(start, 2 * plane_voxels)])
        for i in range(2):
            rotated[first - base + 2 * pair + i] = found[:, i * plane_voxels : (i + 1) * plane_voxels]

    rotations[me] = rotated[pl.ds(half_edge - me - base, orients)]
    pl.semaphore_wait(barrier, group + orients - 2)

    gathers = []
    for step in range(1, group):
        copy = pltpu.make_async_remote_copy(
            src_ref=brick_ref.at[0],
            dst_ref=pencils.at[col_id, row_id],
            send_sem=sems1.at[0, step],
            recv_sem=sems1.at[1, step],
            device_id=brick_peer(step),
            device_id_type=MESH,
        )
        copy.start()
        gathers.append(copy)
    pencils[col_id, row_id] = brick_ref[0]
    parts = brows if orients % brows == 0 else 1
    part_planes = orients // parts
    shares = []
    for step in range(1, orients):
        target = lax.rem(me + step, orients)
        copy = pltpu.make_async_remote_copy(
            src_ref=rotated.at[pl.ds(half_edge - target - base + lax.rem(row_id, parts) * part_planes, part_planes)],
            dst_ref=rotations.at[me, pl.ds(lax.rem(row_id, parts) * part_planes, part_planes)],
            send_sem=sems0.at[0, 0, step],
            recv_sem=sems0.at[0, 1, step],
            device_id=plane_peer(step),
            device_id_type=MESH,
        )
        copy.start()
        shares.append(copy)
    for copy in gathers:
        copy.wait_recv()

    both = None
    for part in range(bcols):
        term = dot(pencils[part].reshape(brows * rows, cols), forward_ref[part])
        both = term if both is None else both + term
    padded = both.shape[1] // 2
    real, imag = both[:, :padded], both[:, padded:]
    weights = lax.rsqrt(dot(real * real + imag * imag, smoothing_ref[...]) + epsilon)
    tall[half_edge : half_edge + brows * rows, :] = dot(
        real * weights, inverse_ref[col_id, :padded, :]
    ) + dot(imag * weights, inverse_ref[col_id, padded:, :])
    start = pl.multiple_of(row_id * rows, 8)
    windows[me] = tall[pl.ds(start, tile_rows), :]
    idle = half_edge // 8 * 8 if brows == 2 else 0
    filled = pl.ds(pl.multiple_of((brows - 1 - row_id) * idle, 8), tile_rows - idle)

    sends = []
    for step in range(1, orients):
        copy = pltpu.make_async_remote_copy(
            src_ref=windows.at[me, filled],
            dst_ref=windows.at[me, filled],
            send_sem=sems2.at[0, step],
            recv_sem=sems2.at[1, step],
            device_id=plane_peer(step),
            device_id_type=MESH,
        )
        copy.start()
        sends.append(copy)

    def unfold(rotation):
        planes = rotations[rotation][:, 0, :]
        lines = jnp.concatenate(
            [planes[:, b * edge : (b + 1) * edge] for b in range(edge)], axis=0
        )
        turned = dot(lines, template_dft_ref[...])
        size = turned.shape[1] // 2
        straight_ref[rotation] = turned[:, :size].reshape(edge, orients, size)
        crossed_ref[rotation] = turned[:, size:].reshape(edge, orients, size)

    unfold(me)

    def share_of(step, turn):
        source = lax.rem(me - step + orients, orients)
        owner = lax.rem(row_id, parts) * part_planes
        block = rotations.at[source, pl.ds(owner, part_planes)]
        to = plane_peer(step)
        if turn:
            to = {"orient": me, "brow": lax.rem(row_id + turn, brows), "bcol": col_id}
        return pltpu.make_async_remote_copy(
            src_ref=block,
            dst_ref=block,
            send_sem=sems0.at[turn, 0, step],
            recv_sem=sems0.at[turn, 1, step],
            device_id=to,
            device_id_type=MESH,
        )

    @pl.loop(1, orients)
    def _(step):
        share_of(step, 0).wait_recv()
        for turn in range(1, parts):
            share_of(step, turn).start()

    @pl.loop(1, orients)
    def _(step):
        for turn in range(1, parts):
            share_of(step, turn).wait()
        unfold(lax.rem(me - step + orients, orients))

    bunch = math.gcd(orients, 8)

    def absorb(plane):
        window = windows[plane]
        gap = plane - me
        near = jnp.logical_and(gap >= -half_edge, gap < half_edge).astype(jnp.float32)
        energy[...] += window * window * near
        transformed = dot(window, volume_dft_ref[...])
        spectrum[...] = transformed
        swapped[...] = pltpu.roll(transformed, transformed.shape[1] // 2, 1)

        def targets(piece):
            lowest = piece * bunch
            held = [totals[lowest + r] for r in range(bunch)]
            for b in range(edge):
                near_part = spectrum[b : b + rows, :]
                far_part = swapped[b : b + rows, :]
                for r in range(bunch):
                    held[r] = held[r] + (
                        near_part * straight_ref[lowest + r, b, pl.ds(plane, 1), :]
                        + far_part * crossed_ref[lowest + r, b, pl.ds(plane, 1), :]
                    )
            for r in range(bunch):
                totals[lowest + r] = held[r]

        if orients == bunch:
            targets(0)
        else:
            pl.loop(0, orients // bunch)(targets)

    absorb(me)

    @pl.loop(1, orients)
    def _(step):
        source = lax.rem(me - step + orients, orients)
        pltpu.make_async_remote_copy(
            src_ref=windows.at[source, filled],
            dst_ref=windows.at[source, filled],
            send_sem=sems2.at[0, step],
            recv_sem=sems2.at[1, step],
            device_id=plane_peer(step),
            device_id_type=MESH,
        ).wait_recv()
        absorb(source)

    summed = energy[0:rows, :]
    for b in range(1, edge):
        summed = summed + energy[b : b + rows, :]
    scaling = lax.rsqrt(dot(summed, box_ref[...]) / voxels + epsilon)
    size = spectrum.shape[1]
    scored = dot(totals[...].reshape(orients * rows, size), score_dft_ref[...])
    best = jnp.max(scored.reshape(orients, rows, cols), axis=0)
    best_ref[0] = best
    scaling_ref[0] = scaling
    for copy in gathers + shares + sends:
        copy.wait_send()


def shards(volume, template, voxel_maps):
    orients, brows, bcols = (lax.axis_size(axis) for axis in ("orient", "brow", "bcol"))
    planes, rows, cols = volume.shape
    edge = template.shape[0]
    half_edge = edge // 2
    voxels = edge**3
    length = cols * bcols
    size = cols + edge
    tile_rows = rows + edge
    base = (half_edge - orients + 1) // 2 * 2
    first = max(0, base)
    last = min(edge, round_up(half_edge + orients, 2))
    held = round_up(half_edge + orients, 2) - base
    group = brows * bcols
    vmem = pl.BlockSpec(memory_space=pltpu.VMEM)
    constants = (
        template_table(edge, size),
        forward_table(length, bcols),
        smoothing_table(length),
        windowed_inverse(length, bcols, half_edge),
        volume_table(size),
        score_table(size, cols),
        box_table(size, cols, edge),
    )
    sizes = (orients, brows, bcols, edge, voxels, base, first, last)
    best, scaling = pl.pallas_call(
        lambda *refs: match_kernel(sizes, *refs),
        out_shape=(jax.ShapeDtypeStruct((1, rows, cols), jnp.float32),) * 2,
        in_specs=[vmem] * 10,
        out_specs=(vmem, vmem),
        scratch_shapes=[
            pltpu.VMEM((edge * edge, edge), jnp.float32),
            pltpu.VMEM((held, 1, edge * edge), jnp.float32),
            pltpu.VMEM((orients, orients, 1, edge * edge), jnp.float32),
            pltpu.VMEM((orients, edge, orients, size), jnp.float32),
            pltpu.VMEM((orients, edge, orients, size), jnp.float32),
            pltpu.VMEM((bcols, brows, rows, cols), jnp.float32),
            pltpu.VMEM((brows * rows + edge, size), jnp.float32),
            pltpu.VMEM((orients, tile_rows, size), jnp.float32),
            pltpu.VMEM((tile_rows, size), jnp.float32),
            pltpu.VMEM((tile_rows, size), jnp.float32),
            pltpu.VMEM((tile_rows, size), jnp.float32),
            pltpu.VMEM((orients, rows, size), jnp.float32),
            pltpu.SemaphoreType.DMA((brows, 2, orients)),
            pltpu.SemaphoreType.DMA((2, group)),
            pltpu.SemaphoreType.DMA((2, orients)),
        ],
        compiler_params=pltpu.CompilerParams(collective_id=0, has_side_effects=True),
        name="match",
    )(volume, template.reshape(edge * edge, edge), voxel_maps, *(jnp.asarray(c) for c in constants))
    return best * scaling


def solution(mesh):
    in_specs = (P("orient", "brow", "bcol"), P(), P("orient", None))
    out_specs = P("orient", "brow", "bcol")
    return jax.shard_map(shards, mesh=mesh, in_specs=in_specs, out_specs=out_specs, check_vma=False)
```

```python
import math

import numpy as np
import jax
import jax.numpy as jnp
from jax import lax
from jax.experimental import pallas as pl
from jax.experimental.pallas import tpu as pltpu
from jax.sharding import PartitionSpec as P

epsilon = 1e-06
floor_share = 0.1
highest = lax.Precision.HIGHEST
LANES = 128
MESH = pl.DeviceIdType.MESH


def round_up(value, step):
    return -(-value // step) * step


def forward_table(length, parts):
    half = length // 2 + 1
    padded = round_up(half, LANES)
    angles = 2.0 * np.pi * (np.outer(np.arange(length), np.arange(half)) % length) / length
    table = np.zeros((length, 2 * padded))
    table[:, :half] = np.cos(angles)
    table[:, padded : padded + half] = -np.sin(angles)
    return table.reshape(parts, length // parts, 2 * padded).astype(np.float32)


def smoothing_table(length):
    half = length // 2 + 1
    padded = round_up(half, LANES)
    table = np.zeros((padded, padded))
    fold = np.minimum(np.arange(length), length - np.arange(length))
    for k in range(half):
        for shift in (-1, 0, 1):
            table[fold[(k + shift) % length], k] += 1.0 / 3.0
        for other in range(length):
            table[fold[other], k] += floor_share / length
    return table.astype(np.float32)


def windowed_inverse(length, parts, margin):
    half = length // 2 + 1
    padded = round_up(half, LANES)
    width = length // parts
    tables = np.zeros((parts, 2 * padded, width + 2 * margin))
    k = np.arange(half)
    share = np.where((k == 0) | (2 * k == length), 1.0, 2.0)[:, None] / math.sqrt(length)
    for part in range(parts):
        columns = np.arange(width + 2 * margin) + part * width - margin
        inside = (columns >= 0) & (columns < length)
        angles = 2.0 * np.pi * (np.outer(k, columns) % length) / length
        tables[part, :half] = share * np.cos(angles) * inside
        tables[part, padded : padded + half] = -share * np.sin(angles) * inside
    return tables.astype(np.float32)


def packed_dft(count, size):
    k = np.arange(size)
    real = k <= size // 2
    freq = np.where(real, k, k - size // 2)
    angles = 2.0 * np.pi * (np.outer(np.arange(count), freq) % size) / size
    return angles, real, freq


def volume_table(size):
    angles, real, freq = packed_dft(size, size)
    return np.where(real, np.cos(angles), -np.sin(angles)).astype(np.float32)


def template_table(count, size):
    angles, real, freq = packed_dft(count, size)
    straight = np.cos(angles)
    edge = (freq == 0) | (freq == size // 2)
    crossed = np.where(real, -np.sin(angles), np.sin(angles)) * ~edge
    return np.concatenate([straight, crossed], axis=1).astype(np.float32)


def score_table(size, count):
    angles, real, freq = packed_dft(count, size)
    share = np.where((freq == 0) | (freq == size // 2), 1.0, 2.0)
    return (np.where(real, np.cos(angles), -np.sin(angles)) * share / size).T.astype(np.float32)


def box_table(size, count, edge):
    offsets = np.arange(size)[:, None] - np.arange(count)[None, :]
    return ((offsets >= 0) & (offsets < edge)).astype(np.float32)


def dot(a, b):
    return jnp.dot(a, b, precision=highest, preferred_element_type=jnp.float32)


def split_table(template_ref, normed):
    lines, edge = template_ref.shape
    template = template_ref[...]
    centred = template - jnp.sum(template, keepdims=True) / (lines * edge)
    normed[...] = centred / jnp.sqrt(jnp.sum(centred * centred, keepdims=True) + epsilon)
    table = jnp.concatenate([normed[pl.ds(j, lines // 8, stride=8), :] for j in range(8)], axis=1)
    spare = round_up(lines // 8, 16) - lines // 8
    table = jnp.concatenate([table, jnp.zeros((spare, 8 * edge), jnp.float32)], axis=0)
    upper = table.astype(jnp.bfloat16)
    lower = (table - upper.astype(jnp.float32)).astype(jnp.bfloat16)
    return jnp.concatenate([upper, lower], axis=0)


def look_up(pieces, index):
    count, span = pieces.shape
    width = index.shape[1]
    high = ((index.astype(jnp.float32) + 0.5) * (1.0 / span)).astype(jnp.int32)
    low = index - high * span
    chosen = lax.broadcasted_iota(jnp.int32, (span, width), 0) == low
    lanes = jnp.dot(
        pieces,
        jnp.where(chosen, 1.0, 0.0).astype(jnp.bfloat16),
        preferred_element_type=jnp.float32,
    )
    lanes = lanes[: count // 2] + lanes[count // 2 :]
    mine = lax.broadcasted_iota(jnp.int32, lanes.shape, 0) == high
    return jnp.sum(jnp.where(mine, lanes, 0.0), axis=0, keepdims=True)


def match_kernel(
    sizes,
    fetch,
    brick_ref,
    template_ref,
    index_ref,
    template_dft_ref,
    forward_ref,
    smoothing_ref,
    inverse_ref,
    volume_dft_ref,
    score_dft_ref,
    box_ref,
    best_ref,
    scaling_ref,
    normed,
    rotated,
    rotations,
    straight_ref,
    crossed_ref,
    pencils,
    tall,
    windows,
    spectrum,
    swapped,
    energy,
    totals,
    sems0,
    sems1,
    sems2,
):
    orients, brows, bcols, edge, voxels, base, first, last = sizes
    half_edge = edge // 2
    rows, cols = brick_ref.shape[1:]
    tile_rows = windows.shape[1]
    me = lax.axis_index("orient")
    row_id = lax.axis_index("brow")
    col_id = lax.axis_index("bcol")
    group = brows * bcols
    place = row_id * bcols + col_id

    def brick_peer(step):
        other = lax.rem(place + step, group)
        return {"orient": me, "brow": other // bcols, "bcol": lax.rem(other, bcols)}

    def partner(step):
        assert orients & (orients - 1) == 0
        other, weight = 0, 1
        while weight < orients:
            other = other + lax.rem(me // weight + step // weight, 2) * weight
            weight *= 2
        return other

    def plane_peer(step):
        return {"orient": partner(step), "brow": row_id, "bcol": col_id}

    windows[...] = jnp.zeros_like(windows)
    barrier = pltpu.get_barrier_semaphore()
    for step in range(1, group):
        pl.semaphore_signal(barrier, inc=1, device_id=brick_peer(step), device_id_type=MESH)
    for step in range(1, orients):
        pl.semaphore_signal(barrier, inc=1, device_id=plane_peer(step), device_id_type=MESH)

    fetch()
    energy[...] = jnp.zeros_like(energy)
    totals[...] = jnp.zeros_like(totals)
    tall[...] = jnp.zeros_like(tall)
    if first > base or last < base + rotated.shape[0]:
        rotated[...] = jnp.zeros_like(rotated)
    pieces = split_table(template_ref, normed)

    pl.semaphore_wait(barrier, group + orients - 2)

    gathers = []
    for step in range(1, group):
        copy = pltpu.make_async_remote_copy(
            src_ref=brick_ref.at[0],
            dst_ref=pencils.at[col_id, row_id],
            send_sem=sems1.at[0, step],
            recv_sem=sems1.at[1, step],
            device_id=brick_peer(step),
            device_id_type=MESH,
        )
        copy.start()
        gathers.append(copy)
    pencils[col_id, row_id] = brick_ref[0]
    plane_voxels = edge * edge

    @pl.loop(0, (last - first) // 2)
    def _(pair):
        start = pl.multiple_of((first + 2 * pair) * plane_voxels, 2 * plane_voxels)
        found = look_up(pieces, index_ref[0:1, pl.ds(start, 2 * plane_voxels)])
        for i in range(2):
            rotated[first - base + 2 * pair + i] = found[:, i * plane_voxels : (i + 1) * plane_voxels]

    rotations[me] = rotated[pl.ds(half_edge - me - base, orients)]
    parts = brows if orients % brows == 0 else 1
    part_planes = orients // parts
    shares = []
    for step in range(1, orients):
        target = partner(step)
        copy = pltpu.make_async_remote_copy(
            src_ref=rotated.at[pl.ds(half_edge - target - base + lax.rem(row_id, parts) * part_planes, part_planes)],
            dst_ref=rotations.at[me, pl.ds(lax.rem(row_id, parts) * part_planes, part_planes)],
            send_sem=sems0.at[0, 0, step],
            recv_sem=sems0.at[0, 1, step],
            device_id=plane_peer(step),
            device_id_type=MESH,
        )
        copy.start()
        shares.append(copy)
    for copy in gathers:
        copy.wait_recv()

    both = None
    for part in range(bcols):
        term = dot(pencils[part].reshape(brows * rows, cols), forward_ref[part])
        both = term if both is None else both + term
    padded = both.shape[1] // 2
    real, imag = both[:, :padded], both[:, padded:]
    weights = lax.rsqrt(dot(real * real + imag * imag, smoothing_ref[...]) + epsilon)
    tall[half_edge : half_edge + brows * rows, :] = dot(
        real * weights, inverse_ref[col_id, :padded, :]
    ) + dot(imag * weights, inverse_ref[col_id, padded:, :])
    start = pl.multiple_of(row_id * rows, 8)
    windows[me] = tall[pl.ds(start, tile_rows), :]
    idle = half_edge // 8 * 8 if brows == 2 else 0
    filled = pl.ds(pl.multiple_of((brows - 1 - row_id) * idle, 8), tile_rows - idle)

    sends = []
    for step in range(1, orients):
        copy = pltpu.make_async_remote_copy(
            src_ref=windows.at[me, filled],
            dst_ref=windows.at[me, filled],
            send_sem=sems2.at[0, step],
            recv_sem=sems2.at[1, step],
            device_id=plane_peer(step),
            device_id_type=MESH,
        )
        copy.start()
        sends.append(copy)

    def unfold(rotation):
        planes = rotations[rotation][:, 0, :]
        lines = jnp.concatenate(
            [planes[:, b * edge : (b + 1) * edge] for b in range(edge)], axis=0
        )
        turned = dot(lines, template_dft_ref[...])
        size = turned.shape[1] // 2
        straight_ref[rotation] = turned[:, :size].reshape(edge, orients, size)
        crossed_ref[rotation] = turned[:, size:].reshape(edge, orients, size)

    unfold(me)

    def share_of(step, turn):
        source = partner(step)
        owner = lax.rem(row_id, parts) * part_planes
        block = rotations.at[source, pl.ds(owner, part_planes)]
        to = plane_peer(step)
        if turn:
            to = {"orient": me, "brow": lax.rem(row_id + turn, brows), "bcol": col_id}
        return pltpu.make_async_remote_copy(
            src_ref=block,
            dst_ref=block,
            send_sem=sems0.at[turn, 0, step],
            recv_sem=sems0.at[turn, 1, step],
            device_id=to,
            device_id_type=MESH,
        )

    @pl.loop(1, orients)
    def _(step):
        share_of(step, 0).wait_recv()
        for turn in range(1, parts):
            share_of(step, turn).start()

    @pl.loop(1, orients)
    def _(step):
        for turn in range(1, parts):
            share_of(step, turn).wait()
        unfold(partner(step))

    bunch = math.gcd(orients, 8)

    def absorb(plane):
        window = windows[plane]
        gap = plane - me
        near = jnp.logical_and(gap >= -half_edge, gap < half_edge).astype(jnp.float32)
        energy[...] += window * window * near
        transformed = dot(window, volume_dft_ref[...])
        spectrum[...] = transformed
        swapped[...] = pltpu.roll(transformed, transformed.shape[1] // 2, 1)

        def targets(piece):
            lowest = piece * bunch
            held = [totals[lowest + r] for r in range(bunch)]
            for b in range(edge):
                near_part = spectrum[b : b + rows, :]
                far_part = swapped[b : b + rows, :]
                for r in range(bunch):
                    held[r] = held[r] + (
                        near_part * straight_ref[lowest + r, b, pl.ds(plane, 1), :]
                        + far_part * crossed_ref[lowest + r, b, pl.ds(plane, 1), :]
                    )
            for r in range(bunch):
                totals[lowest + r] = held[r]

        if orients == bunch:
            targets(0)
        else:
            pl.loop(0, orients // bunch)(targets)

    absorb(me)

    @pl.loop(1, orients)
    def _(step):
        source = partner(step)
        pltpu.make_async_remote_copy(
            src_ref=windows.at[source, filled],
            dst_ref=windows.at[source, filled],
            send_sem=sems2.at[0, step],
            recv_sem=sems2.at[1, step],
            device_id=plane_peer(step),
            device_id_type=MESH,
        ).wait_recv()
        absorb(source)

    summed = energy[0:rows, :]
    for b in range(1, edge):
        summed = summed + energy[b : b + rows, :]
    scaling = lax.rsqrt(dot(summed, box_ref[...]) / voxels + epsilon)
    size = spectrum.shape[1]
    scored = dot(totals[...].reshape(orients * rows, size), score_dft_ref[...])
    best = jnp.max(scored.reshape(orients, rows, cols), axis=0)
    best_ref[0] = best
    scaling_ref[0] = scaling
    for copy in gathers + shares + sends:
        copy.wait_send()


def staged(sizes, count, *refs):
    sources, results = refs[:count], refs[count : count + 2]
    held, rest = refs[count + 2 : 2 * count + 2], refs[2 * count + 2 : -1]
    copies = [
        pltpu.make_async_copy(source, target, refs[-1].at[i])
        for i, (source, target) in enumerate(zip(sources, held))
    ]
    for copy in copies:
        copy.start()

    def fetch():
        for copy in copies:
            copy.wait()

    match_kernel(sizes, fetch, *held, *results, *rest)


def shards(volume, template, voxel_maps):
    orients, brows, bcols = (lax.axis_size(axis) for axis in ("orient", "brow", "bcol"))
    planes, rows, cols = volume.shape
    edge = template.shape[0]
    half_edge = edge // 2
    voxels = edge**3
    length = cols * bcols
    size = cols + edge
    tile_rows = rows + edge
    base = (half_edge - orients + 1) // 2 * 2
    first = max(0, base)
    last = min(edge, round_up(half_edge + orients, 2))
    held = round_up(half_edge + orients, 2) - base
    group = brows * bcols
    vmem = pl.BlockSpec(memory_space=pltpu.VMEM)
    constants = (
        template_table(edge, size),
        forward_table(length, bcols),
        smoothing_table(length),
        windowed_inverse(length, bcols, half_edge),
        volume_table(size),
        score_table(size, cols),
        box_table(size, cols, edge),
    )
    sizes = (orients, brows, bcols, edge, voxels, base, first, last)
    operands = (volume, template.reshape(edge * edge, edge), voxel_maps)
    operands += tuple(jnp.asarray(c) for c in constants)
    best, scaling = pl.pallas_call(
        lambda *refs: staged(sizes, len(operands), *refs),
        out_shape=(jax.ShapeDtypeStruct((1, rows, cols), jnp.float32),) * 2,
        in_specs=[pl.BlockSpec(memory_space=pl.ANY)] * len(operands),
        out_specs=(vmem, vmem),
        scratch_shapes=[pltpu.VMEM(x.shape, x.dtype) for x in operands]
        + [
            pltpu.VMEM((edge * edge, edge), jnp.float32),
            pltpu.VMEM((held, 1, edge * edge), jnp.float32),
            pltpu.VMEM((orients, orients, 1, edge * edge), jnp.float32),
            pltpu.VMEM((orients, edge, orients, size), jnp.float32),
            pltpu.VMEM((orients, edge, orients, size), jnp.float32),
            pltpu.VMEM((bcols, brows, rows, cols), jnp.float32),
            pltpu.VMEM((brows * rows + edge, size), jnp.float32),
            pltpu.VMEM((orients, tile_rows, size), jnp.float32),
            pltpu.VMEM((tile_rows, size), jnp.float32),
            pltpu.VMEM((tile_rows, size), jnp.float32),
            pltpu.VMEM((tile_rows, size), jnp.float32),
            pltpu.VMEM((orients, rows, size), jnp.float32),
            pltpu.SemaphoreType.DMA((brows, 2, orients)),
            pltpu.SemaphoreType.DMA((2, group)),
            pltpu.SemaphoreType.DMA((2, orients)),
            pltpu.SemaphoreType.DMA((len(operands),)),
        ],
        compiler_params=pltpu.CompilerParams(collective_id=0, has_side_effects=True),
        name="match",
    )(*operands)
    return best * scaling


def solution(mesh):
    in_specs = (P("orient", "brow", "bcol"), P(), P("orient", None))
    out_specs = P("orient", "brow", "bcol")
    return jax.shard_map(shards, mesh=mesh, in_specs=in_specs, out_specs=out_specs, check_vma=False)
```

```python
import math

import numpy as np
import jax
import jax.numpy as jnp
from jax import lax
from jax.experimental import pallas as pl
from jax.experimental.pallas import tpu as pltpu
from jax.sharding import PartitionSpec as P

epsilon = 1e-06
floor_share = 0.1
highest = lax.Precision.HIGHEST
LANES = 128
MESH = pl.DeviceIdType.MESH


def round_up(value, step):
    return -(-value // step) * step


def forward_table(length, parts):
    half = length // 2 + 1
    padded = round_up(half, LANES)
    angles = 2.0 * np.pi * (np.outer(np.arange(length), np.arange(half)) % length) / length
    table = np.zeros((length, 2 * padded))
    table[:, :half] = np.cos(angles)
    table[:, padded : padded + half] = -np.sin(angles)
    return table.reshape(parts, length // parts, 2 * padded).astype(np.float32)


def smoothing_table(length):
    half = length // 2 + 1
    padded = round_up(half, LANES)
    table = np.zeros((padded, padded))
    fold = np.minimum(np.arange(length), length - np.arange(length))
    for k in range(half):
        for shift in (-1, 0, 1):
            table[fold[(k + shift) % length], k] += 1.0 / 3.0
        for other in range(length):
            table[fold[other], k] += floor_share / length
    return table.astype(np.float32)


def windowed_inverse(length, parts, margin):
    half = length // 2 + 1
    padded = round_up(half, LANES)
    width = length // parts
    tables = np.zeros((parts, 2 * padded, width + 2 * margin))
    k = np.arange(half)
    share = np.where((k == 0) | (2 * k == length), 1.0, 2.0)[:, None] / math.sqrt(length)
    for part in range(parts):
        columns = np.arange(width + 2 * margin) + part * width - margin
        inside = (columns >= 0) & (columns < length)
        angles = 2.0 * np.pi * (np.outer(k, columns) % length) / length
        tables[part, :half] = share * np.cos(angles) * inside
        tables[part, padded : padded + half] = -share * np.sin(angles) * inside
    return tables.astype(np.float32)


def packed_dft(count, size):
    k = np.arange(size)
    real = k <= size // 2
    freq = np.where(real, k, k - size // 2)
    angles = 2.0 * np.pi * (np.outer(np.arange(count), freq) % size) / size
    return angles, real, freq


def volume_table(size):
    angles, real, freq = packed_dft(size, size)
    return np.where(real, np.cos(angles), -np.sin(angles)).astype(np.float32)


def template_table(count, size):
    angles, real, freq = packed_dft(count, size)
    straight = np.cos(angles)
    edge = (freq == 0) | (freq == size // 2)
    crossed = np.where(real, -np.sin(angles), np.sin(angles)) * ~edge
    return np.concatenate([straight, crossed], axis=1).astype(np.float32)


def score_table(size, count):
    angles, real, freq = packed_dft(count, size)
    share = np.where((freq == 0) | (freq == size // 2), 1.0, 2.0)
    return (np.where(real, np.cos(angles), -np.sin(angles)) * share / size).T.astype(np.float32)


def box_table(size, count, edge):
    offsets = np.arange(size)[:, None] - np.arange(count)[None, :]
    return ((offsets >= 0) & (offsets < edge)).astype(np.float32)


def dot(a, b):
    return jnp.dot(a, b, precision=highest, preferred_element_type=jnp.float32)


def split_table(template_ref, normed):
    lines, edge = template_ref.shape
    template = template_ref[...]
    centred = template - jnp.sum(template, keepdims=True) / (lines * edge)
    normed[...] = centred / jnp.sqrt(jnp.sum(centred * centred, keepdims=True) + epsilon)
    table = jnp.concatenate([normed[pl.ds(j, lines // 8, stride=8), :] for j in range(8)], axis=1)
    spare = round_up(lines // 8, 16) - lines // 8
    table = jnp.concatenate([table, jnp.zeros((spare, 8 * edge), jnp.float32)], axis=0)
    upper = table.astype(jnp.bfloat16)
    lower = (table - upper.astype(jnp.float32)).astype(jnp.bfloat16)
    return jnp.concatenate([upper, lower], axis=0)


def look_up(pieces, index):
    count, span = pieces.shape
    width = index.shape[1]
    high = ((index.astype(jnp.float32) + 0.5) * (1.0 / span)).astype(jnp.int32)
    low = index - high * span
    chosen = lax.broadcasted_iota(jnp.int32, (span, width), 0) == low
    lanes = jnp.dot(
        pieces,
        jnp.where(chosen, 1.0, 0.0).astype(jnp.bfloat16),
        preferred_element_type=jnp.float32,
    )
    lanes = lanes[: count // 2] + lanes[count // 2 :]
    mine = lax.broadcasted_iota(jnp.int32, lanes.shape, 0) == high
    return jnp.sum(jnp.where(mine, lanes, 0.0), axis=0, keepdims=True)


def match_kernel(
    sizes,
    fetch,
    brick_ref,
    template_ref,
    index_ref,
    template_dft_ref,
    forward_ref,
    smoothing_ref,
    inverse_ref,
    volume_dft_ref,
    score_dft_ref,
    box_ref,
    best_ref,
    scaling_ref,
    normed,
    rotated,
    rotations,
    straight_ref,
    crossed_ref,
    pencils,
    tall,
    windows,
    spectrum,
    swapped,
    energy,
    totals,
    sems0,
    sems1,
    sems2,
):
    orients, brows, bcols, edge, voxels, base, first, last = sizes
    half_edge = edge // 2
    rows, cols = brick_ref.shape[1:]
    tile_rows = windows.shape[1]
    me = lax.axis_index("orient")
    row_id = lax.axis_index("brow")
    col_id = lax.axis_index("bcol")
    group = brows * bcols
    place = row_id * bcols + col_id

    def brick_peer(step):
        other = lax.rem(place + step, group)
        return {"orient": me, "brow": other // bcols, "bcol": lax.rem(other, bcols)}

    def partner(step):
        assert orients & (orients - 1) == 0
        other, weight = 0, 1
        while weight < orients:
            other = other + lax.rem(me // weight + step // weight, 2) * weight
            weight *= 2
        return other

    def plane_peer(step):
        return {"orient": partner(step), "brow": row_id, "bcol": col_id}

    windows[...] = jnp.zeros_like(windows)
    barrier = pltpu.get_barrier_semaphore()
    for step in range(1, group):
        pl.semaphore_signal(barrier, inc=1, device_id=brick_peer(step), device_id_type=MESH)
    for step in range(1, orients):
        pl.semaphore_signal(barrier, inc=1, device_id=plane_peer(step), device_id_type=MESH)

    fetch()
    energy[...] = jnp.zeros_like(energy)
    totals[...] = jnp.zeros_like(totals)
    tall[...] = jnp.zeros_like(tall)
    if first > base or last < base + rotated.shape[0]:
        rotated[...] = jnp.zeros_like(rotated)
    pieces = split_table(template_ref, normed)

    pl.semaphore_wait(barrier, group + orients - 2)

    gathers = []
    for step in range(1, group):
        copy = pltpu.make_async_remote_copy(
            src_ref=brick_ref.at[0],
            dst_ref=pencils.at[col_id, row_id],
            send_sem=sems1.at[0, step],
            recv_sem=sems1.at[1, step],
            device_id=brick_peer(step),
            device_id_type=MESH,
        )
        copy.start()
        gathers.append(copy)
    pencils[col_id, row_id] = brick_ref[0]
    plane_voxels = edge * edge

    @pl.loop(0, (last - first) // 2)
    def _(pair):
        start = pl.multiple_of((first + 2 * pair) * plane_voxels, 2 * plane_voxels)
        found = look_up(pieces, index_ref[0:1, pl.ds(start, 2 * plane_voxels)])
        for i in range(2):
            rotated[first - base + 2 * pair + i] = found[:, i * plane_voxels : (i + 1) * plane_voxels]

    rotations[me] = rotated[pl.ds(half_edge - me - base, orients)]
    parts = brows if orients % brows == 0 else 1
    part_planes = orients // parts
    shares = []
    for step in range(1, orients):
        target = partner(step)
        copy = pltpu.make_async_remote_copy(
            src_ref=rotated.at[pl.ds(half_edge - target - base + lax.rem(row_id, parts) * part_planes, part_planes)],
            dst_ref=rotations.at[me, pl.ds(lax.rem(row_id, parts) * part_planes, part_planes)],
            send_sem=sems0.at[0, 0, step],
            recv_sem=sems0.at[0, 1, step],
            device_id=plane_peer(step),
            device_id_type=MESH,
        )
        copy.start()
        shares.append(copy)
    for copy in gathers:
        copy.wait_recv()

    both = None
    for part in range(bcols):
        term = dot(pencils[part].reshape(brows * rows, cols), forward_ref[part])
        both = term if both is None else both + term
    padded = both.shape[1] // 2
    real, imag = both[:, :padded], both[:, padded:]
    weights = lax.rsqrt(dot(real * real + imag * imag, smoothing_ref[...]) + epsilon)
    tall[half_edge : half_edge + brows * rows, :] = dot(
        real * weights, inverse_ref[col_id, :padded, :]
    ) + dot(imag * weights, inverse_ref[col_id, padded:, :])
    start = pl.multiple_of(row_id * rows, 8)
    windows[me] = tall[pl.ds(start, tile_rows), :]
    idle = half_edge // 8 * 8 if brows == 2 else 0
    filled = pl.ds(pl.multiple_of((brows - 1 - row_id) * idle, 8), tile_rows - idle)

    sends = []
    for step in range(1, orients):
        copy = pltpu.make_async_remote_copy(
            src_ref=windows.at[me, filled],
            dst_ref=windows.at[me, filled],
            send_sem=sems2.at[0, step],
            recv_sem=sems2.at[1, step],
            device_id=plane_peer(step),
            device_id_type=MESH,
        )
        copy.start()
        sends.append(copy)

    def unfold(rotation):
        planes = rotations[rotation][:, 0, :]
        lines = jnp.concatenate(
            [planes[:, b * edge : (b + 1) * edge] for b in range(edge)], axis=0
        )
        turned = dot_short(lines, template_dft_ref[...])
        size = turned.shape[1] // 2
        straight_ref[rotation] = turned[:, :size].reshape(edge, orients, size)
        crossed_ref[rotation] = turned[:, size:].reshape(edge, orients, size)

    unfold(me)

    def share_of(step, turn):
        source = partner(step)
        owner = lax.rem(row_id, parts) * part_planes
        block = rotations.at[source, pl.ds(owner, part_planes)]
        to = plane_peer(step)
        if turn:
            to = {"orient": me, "brow": lax.rem(row_id + turn, brows), "bcol": col_id}
        return pltpu.make_async_remote_copy(
            src_ref=block,
            dst_ref=block,
            send_sem=sems0.at[turn, 0, step],
            recv_sem=sems0.at[turn, 1, step],
            device_id=to,
            device_id_type=MESH,
        )

    @pl.loop(1, orients)
    def _(step):
        share_of(step, 0).wait_recv()
        for turn in range(1, parts):
            share_of(step, turn).start()

    @pl.loop(1, orients)
    def _(step):
        for turn in range(1, parts):
            share_of(step, turn).wait()
        unfold(partner(step))

    bunch = math.gcd(orients, 8)

    def absorb(plane):
        window = windows[plane]
        gap = plane - me
        near = jnp.logical_and(gap >= -half_edge, gap < half_edge).astype(jnp.float32)
        energy[...] += window * window * near
        transformed = dot_short(window, volume_dft_ref[...])
        spectrum[...] = transformed
        swapped[...] = pltpu.roll(transformed, transformed.shape[1] // 2, 1)

        def targets(piece):
            lowest = piece * bunch
            held = [totals[lowest + r] for r in range(bunch)]
            for b in range(edge):
                near_part = spectrum[b : b + rows, :]
                far_part = swapped[b : b + rows, :]
                for r in range(bunch):
                    held[r] = held[r] + (
                        near_part * straight_ref[lowest + r, b, pl.ds(plane, 1), :]
                        + far_part * crossed_ref[lowest + r, b, pl.ds(plane, 1), :]
                    )
            for r in range(bunch):
                totals[lowest + r] = held[r]

        if orients == bunch:
            targets(0)
        else:
            pl.loop(0, orients // bunch)(targets)

    absorb(me)

    @pl.loop(1, orients)
    def _(step):
        source = partner(step)
        pltpu.make_async_remote_copy(
            src_ref=windows.at[source, filled],
            dst_ref=windows.at[source, filled],
            send_sem=sems2.at[0, step],
            recv_sem=sems2.at[1, step],
            device_id=plane_peer(step),
            device_id_type=MESH,
        ).wait_recv()
        absorb(source)

    summed = energy[0:rows, :]
    for b in range(1, edge):
        summed = summed + energy[b : b + rows, :]
    scaling = lax.rsqrt(dot(summed, box_ref[...]) / voxels + epsilon)
    size = spectrum.shape[1]
    scored = dot_short(totals[...].reshape(orients * rows, size), score_dft_ref[...])
    best = jnp.max(scored.reshape(orients, rows, cols), axis=0)
    best_ref[0] = best
    scaling_ref[0] = scaling
    for copy in gathers + shares + sends:
        copy.wait_send()


def dot_short(a, b):
    return jnp.dot(a, b, precision=lax.Precision.HIGH, preferred_element_type=jnp.float32)


def staged(sizes, count, *refs):
    sources, results = refs[:count], refs[count : count + 2]
    held, rest = refs[count + 2 : 2 * count + 2], refs[2 * count + 2 : -1]
    copies = [
        pltpu.make_async_copy(source, target, refs[-1].at[i])
        for i, (source, target) in enumerate(zip(sources, held))
    ]
    for copy in copies:
        copy.start()

    def fetch():
        for copy in copies:
            copy.wait()

    match_kernel(sizes, fetch, *held, *results, *rest)


def shards(volume, template, voxel_maps):
    orients, brows, bcols = (lax.axis_size(axis) for axis in ("orient", "brow", "bcol"))
    planes, rows, cols = volume.shape
    edge = template.shape[0]
    half_edge = edge // 2
    voxels = edge**3
    length = cols * bcols
    size = cols + edge
    tile_rows = rows + edge
    base = (half_edge - orients + 1) // 2 * 2
    first = max(0, base)
    last = min(edge, round_up(half_edge + orients, 2))
    held = round_up(half_edge + orients, 2) - base
    group = brows * bcols
    vmem = pl.BlockSpec(memory_space=pltpu.VMEM)
    constants = (
        template_table(edge, size),
        forward_table(length, bcols),
        smoothing_table(length),
        windowed_inverse(length, bcols, half_edge),
        volume_table(size),
        score_table(size, cols),
        box_table(size, cols, edge),
    )
    sizes = (orients, brows, bcols, edge, voxels, base, first, last)
    operands = (volume, template.reshape(edge * edge, edge), voxel_maps)
    operands += tuple(jnp.asarray(c) for c in constants)
    best, scaling = pl.pallas_call(
        lambda *refs: staged(sizes, len(operands), *refs),
        out_shape=(jax.ShapeDtypeStruct((1, rows, cols), jnp.float32),) * 2,
        in_specs=[pl.BlockSpec(memory_space=pl.ANY)] * len(operands),
        out_specs=(vmem, vmem),
        scratch_shapes=[pltpu.VMEM(x.shape, x.dtype) for x in operands]
        + [
            pltpu.VMEM((edge * edge, edge), jnp.float32),
            pltpu.VMEM((held, 1, edge * edge), jnp.float32),
            pltpu.VMEM((orients, orients, 1, edge * edge), jnp.float32),
            pltpu.VMEM((orients, edge, orients, size), jnp.float32),
            pltpu.VMEM((orients, edge, orients, size), jnp.float32),
            pltpu.VMEM((bcols, brows, rows, cols), jnp.float32),
            pltpu.VMEM((brows * rows + edge, size), jnp.float32),
            pltpu.VMEM((orients, tile_rows, size), jnp.float32),
            pltpu.VMEM((tile_rows, size), jnp.float32),
            pltpu.VMEM((tile_rows, size), jnp.float32),
            pltpu.VMEM((tile_rows, size), jnp.float32),
            pltpu.VMEM((orients, rows, size), jnp.float32),
            pltpu.SemaphoreType.DMA((brows, 2, orients)),
            pltpu.SemaphoreType.DMA((2, group)),
            pltpu.SemaphoreType.DMA((2, orients)),
            pltpu.SemaphoreType.DMA((len(operands),)),
        ],
        compiler_params=pltpu.CompilerParams(collective_id=0, has_side_effects=True),
        name="match",
    )(*operands)
    return best * scaling


def solution(mesh):
    in_specs = (P("orient", "brow", "bcol"), P(), P("orient", None))
    out_specs = P("orient", "brow", "bcol")
    return jax.shard_map(shards, mesh=mesh, in_specs=in_specs, out_specs=out_specs, check_vma=False)
```
